256 devices in a mesh: shock: 32 (over z, x), trans: 8 (over y, core).
Axes of the slice: x: 4, y: 4, z: 8, core: 2. Of those that a mesh axis runs over, the one named last changes fastest.
Arguments:
- conserved: float32 [11, 10, 524288], P(None, None, ('shock', 'trans')), may hold values from -6 to 6
- cell_size: float32 [524288], P(('shock', 'trans')), may hold values from 0.5 to 2
- sound_speed: float32 [524288], P(('shock', 'trans')), may hold values from 0.3 to 1.8
- jacobian: float32 [3, 11, 11], replicated, may hold values from -1.75 to 1.75
- derivative: float32 [3, 10, 10], replicated, may hold values from -2 to 2
- restriction: float32 [4, 6, 10], replicated, may hold values from -2 to 2
- lifting: float32 [4, 10, 6], replicated, may hold values from -2.5 to 2.5
- vertex_velocity: float32 [3, 131072], P(None, ('shock', 'trans')), may hold values from -1.8 to 1.8
- share_index: int32 [2, 32768], P(None, ('shock', 'trans')), may hold values from 0 to 511
- elem_vertex: int32 [4, 524288], P(None, ('shock', 'trans')), may hold values from 0 to 767
- inner_elem: int32 [2, 1048576], P(None, ('shock', 'trans')), may hold values from 0 to 2047
- inner_face: int32 [2, 1048576], P(None, ('shock', 'trans')), may hold values from 0 to 3
- inner_normal: float32 [3, 1048576], P(None, ('shock', 'trans')), may hold values from -3 to 3
- slab_elem: int32 [2, 65536], P(None, ('shock', 'trans')), may hold values from 0 to 2047
- slab_face: int32 [2, 65536], P(None, ('shock', 'trans')), may hold values from 0 to 3
- slab_normal: float32 [3, 2, 65536], P(None, None, ('shock', 'trans')), may hold values from -3 to 3
- peer_elem: int32 [8, 16384], P(None, ('shock', 'trans')), may hold values from 0 to 2047
- peer_face: int32 [8, 16384], P(None, ('shock', 'trans')), may hold values from 0 to 3
- peer_normal: float32 [3, 8, 16384], P(None, None, ('shock', 'trans')), may hold values from -3 to 3
- peer_count: int32 [8, 256], P(None, ('shock', 'trans')), may hold values from 0 to 64, as said below
Outputs:
- rate: float32 [11, 10, 524288], P(None, None, ('shock', 'trans'))
- step_size: float32 [], replicated
The draws below stay inside these ranges and needn't reach their ends.
Inputs may be any that keep to these rules, and one draw needn't show every extreme that they name: peer_count[q, p] is the same for partition p at trans position q' and the partition of the same slab at position q when read from the other side, is 0 for q equal to p's own position, and equals 64 for some pair of each slab; slots at or past it are padding.
All inputs are finite; a program needn't handle non-finite values.
Results may differ from the reference program's by a relative error of at most 0.0003.
Values sent between devices are 32-bit elements; how exact they have to be, the bound alone decides.
No kernel may reach another device: no remote copies, remote signals or barrier semaphores. Data moves between devices by JAX's collectives and lax.ppermute only.
A program may use at most 128 MiB of HBM per device.

```python
import math
import jax
import jax.numpy as jnp
from jax import lax

VARS = 11
BASIS = 10
FACE_BASIS = 6
EL_DEV = 2048
SLABS = 32
PEERS = 8
PARTITIONS = 256
ELEMS = 524288
SLAB_FACES = 256
PEER_FACES = 64
OWN_VERTS = 512
SHARED_VERTS = 128
INNER_FACES = 4096


def draw_sound_speed(key, part):
    position = jnp.arange(ELEMS, dtype=jnp.float32) / ELEMS
    spread = 0.3 * jnp.exp(jax.random.uniform(key, (ELEMS,), jnp.float32, 0.0, math.log(2.0)))
    return spread * jnp.exp(position * math.log(3.0))


def draw_peer_count(key, part):
    key_list = jax.random.split(key, 4)
    counts = jax.random.randint(key_list[0], (SLABS, PEERS, PEERS), PEER_FACES // 2, PEER_FACES + 1)
    living = jax.random.randint(key_list[1], (SLABS, PEERS, PEERS), 0, 5) < 4
    counts = jnp.where(living, counts, 0)
    grid_index = jnp.arange(PEERS)
    above_diag = grid_index[:, None] < grid_index[None, :]
    counts = jnp.where(above_diag[None], counts, jnp.swapaxes(counts, 1, 2))
    counts = jnp.where((grid_index[:, None] == grid_index[None, :])[None], 0, counts)
    first_peer = jax.random.randint(key_list[2], (SLABS,), 0, PEERS)
    second_peer = (first_peer + 1 + jax.random.randint(key_list[3], (SLABS,), 0, PEERS - 1)) % PEERS
    row_index = grid_index[None, :, None]
    col_index = grid_index[None, None, :]
    paired = (row_index == first_peer[:, None, None]) & (col_index == second_peer[:, None, None]) | (row_index == second_peer[:, None, None]) & (col_index == first_peer[:, None, None])
    counts = jnp.where(paired, PEER_FACES, counts)
    return jnp.transpose(counts, (2, 0, 1)).reshape(PEERS, SLABS * PEERS).astype(jnp.int32)


def place_ends(array, own_key, low, largest):
    longest = array.shape.index(max(array.shape))
    spots = []
    for shift in (0, 1):
        where = [jax.random.randint(jax.random.fold_in(own_key, axis), (), 0, length) for axis, length in enumerate(array.shape)]
        where[longest] = (where[longest] + shift) % array.shape[longest]
        spots.append(tuple(where))
    return array.at[spots[0]].set(low).at[spots[1]].set(largest)


def level_of(rng, extent, shards, low, largest):
    gain, own = 1.0, jax.random.fold_in(rng, 6)
    for dim, blocks in shards:
        draws = jnp.exp(jax.random.uniform(jax.random.fold_in(own, dim), (blocks,), jnp.float32, low / len(shards), largest / len(shards)))
        gain = gain * jnp.repeat(draws, extent[dim] // blocks).reshape([-1 if axis == dim else 1 for axis in range(len(extent))])
    return gain


def scatter_about(key, extent, deviation, limit, cuts=(), held_as=jnp.bfloat16):
    values = deviation * jax.random.normal(key, extent, jnp.float32)
    if cuts:
        values = values * level_of(key, extent, cuts, -0.22, 0.18)
    return jnp.clip(values, -limit, limit).astype(held_as)


def setup_inputs(seed: int = 0) -> dict:
    arg_keys = jax.random.split(jax.random.key(seed), 21)
    return {
        "conserved": scatter_about(arg_keys[0], (VARS, BASIS, ELEMS), 1.0, 6.0, ((2, 256),), jnp.float32),
        "cell_size": jnp.clip(jnp.exp(math.log(2.0) - 1.3862944 * jax.random.uniform(arg_keys[1], (ELEMS,), jnp.float32) ** level_of(arg_keys[1], (ELEMS,), ((0, 256),), -0.2, 0.2)), 0.5, 2.0),
        "sound_speed": draw_sound_speed(jax.random.fold_in(arg_keys[20], 71), 0),
        "jacobian": scatter_about(arg_keys[3], (3, VARS, VARS), VARS ** -0.5, 1.75, (), jnp.float32),
        "derivative": scatter_about(arg_keys[4], (3, BASIS, BASIS), BASIS ** -0.5, 2.0, (), jnp.float32),
        "restriction": scatter_about(arg_keys[5], (4, FACE_BASIS, BASIS), BASIS ** -0.5, 2.0, (), jnp.float32),
        "lifting": scatter_about(arg_keys[6], (4, BASIS, FACE_BASIS), FACE_BASIS ** -0.5, 2.5, (), jnp.float32),
        "vertex_velocity": scatter_about(arg_keys[7], (3, OWN_VERTS * PARTITIONS), 0.3, 1.8, ((1, 256),), jnp.float32),
        "share_index": place_ends(jax.random.randint(arg_keys[8], (2, SHARED_VERTS * PARTITIONS), 0, OWN_VERTS), jax.random.fold_in(arg_keys[8], 1), 0, OWN_VERTS - 1).astype(jnp.int32),
        "elem_vertex": place_ends(jax.random.randint(arg_keys[9], (4, ELEMS), 0, OWN_VERTS + 2 * SHARED_VERTS), jax.random.fold_in(arg_keys[9], 1), 0, (OWN_VERTS + 2 * SHARED_VERTS) - 1).astype(jnp.int32),
        "inner_elem": place_ends(jax.random.randint(arg_keys[10], (2, INNER_FACES * PARTITIONS), 0, EL_DEV), jax.random.fold_in(arg_keys[10], 1), 0, EL_DEV - 1).astype(jnp.int32),
        "inner_face": place_ends(jax.random.randint(arg_keys[11], (2, INNER_FACES * PARTITIONS), 0, 4), jax.random.fold_in(arg_keys[11], 1), 0, 3).astype(jnp.int32),
        "inner_normal": scatter_about(arg_keys[12], (3, INNER_FACES * PARTITIONS), 0.6, 3.0, ((1, 256),), jnp.float32),
        "slab_elem": place_ends(jax.random.randint(arg_keys[13], (2, SLAB_FACES * PARTITIONS), 0, EL_DEV), jax.random.fold_in(arg_keys[13], 1), 0, EL_DEV - 1).astype(jnp.int32),
        "slab_face": place_ends(jax.random.randint(arg_keys[14], (2, SLAB_FACES * PARTITIONS), 0, 4), jax.random.fold_in(arg_keys[14], 1), 0, 3).astype(jnp.int32),
        "slab_normal": scatter_about(arg_keys[15], (3, 2, SLAB_FACES * PARTITIONS), 0.6, 3.0, ((2, 256),), jnp.float32),
        "peer_elem": place_ends(jax.random.randint(arg_keys[16], (PEERS, PEER_FACES * PARTITIONS), 0, EL_DEV), jax.random.fold_in(arg_keys[16], 1), 0, EL_DEV - 1).astype(jnp.int32),
        "peer_face": place_ends(jax.random.randint(arg_keys[17], (PEERS, PEER_FACES * PARTITIONS), 0, 4), jax.random.fold_in(arg_keys[17], 1), 0, 3).astype(jnp.int32),
        "peer_normal": scatter_about(arg_keys[18], (3, PEERS, PEER_FACES * PARTITIONS), 0.6, 3.0, ((2, 256),), jnp.float32),
        "peer_count": draw_peer_count(jax.random.fold_in(arg_keys[20], 71), 0),
    }


HIGHEST_PREC = lax.Precision.HIGHEST
CFL_NUMBER = 0.3


def spatial(coeffs, mesh_vel, cell_scale, jacobian, derivative):
    summed = jnp.zeros_like(coeffs)
    for axis_dim in range(3):
        differentiated = jnp.einsum('vbe,cb->vce', coeffs, derivative[axis_dim], precision=HIGHEST_PREC)
        summed = summed + jnp.einsum('uv,vce->uce', jacobian[axis_dim], differentiated, precision=HIGHEST_PREC) - mesh_vel[axis_dim][None, None, :] * differentiated
    return summed / cell_scale[None, None, :]


def predict(coeffs, mesh_vel, cell_scale, step_size, jacobian, derivative):
    first_term = spatial(coeffs, mesh_vel, cell_scale, jacobian, derivative)
    second = spatial(first_term, mesh_vel, cell_scale, jacobian, derivative)
    return coeffs - (0.5 * step_size) * first_term + (step_size * step_size / 6.0) * second


def all_traces(predicted, restriction):
    num_vars = predicted.shape[0]
    elem_count = predicted.shape[2]
    face_table = jnp.einsum('kfb,vbe->vfke', restriction, predicted, precision=HIGHEST_PREC)
    return face_table.reshape(num_vars * restriction.shape[1], 4 * elem_count)


def pick(face_table, bound_row, elem_ids, face_ids, elem_count):
    return jnp.concatenate([face_table[:, face_ids * elem_count + elem_ids], bound_row[elem_ids][None, :]], axis=0)


def riemann(own_trace, theirs, normal, jacobian, face_basis):
    num_vars = jacobian.shape[1]
    face_count = own_trace.shape[1]
    inside = own_trace[:-1].reshape(num_vars, face_basis, face_count)
    outside = theirs[:-1].reshape(num_vars, face_basis, face_count)
    bound_max = jnp.maximum(own_trace[-1], theirs[-1])
    jump_value = outside - inside
    normal_flux = jnp.zeros_like(jump_value)
    for axis_dim in range(3):
        normal_flux = normal_flux + normal[axis_dim][None, None, :] * jnp.einsum('uv,vfn->ufn', jacobian[axis_dim], jump_value, precision=HIGHEST_PREC)
    return (0.5 * (normal_flux - bound_max[None, None, :] * jump_value)).reshape(num_vars * face_basis, face_count)


def face_rate(columns, values, lifting, num_vars, face_basis, elem_count):
    buffer = jnp.zeros((num_vars * face_basis, 4 * elem_count), jnp.float32).at[:, columns].add(values)
    return jnp.einsum('kbf,vfke->vbe', lifting, buffer.reshape(num_vars, face_basis, 4, elem_count), precision=HIGHEST_PREC)


def reference(conserved, cell_size, sound_speed, jacobian, derivative, restriction, lifting, vertex_velocity, share_index, elem_vertex, inner_elem, inner_face, inner_normal, slab_elem, slab_face, slab_normal, peer_elem, peer_face, peer_normal, peer_count):
    partitions = PARTITIONS
    elem_count = EL_DEV
    face_basis = FACE_BASIS
    num_vars = VARS
    states = jnp.moveaxis(conserved.reshape(VARS, BASIS, partitions, elem_count), 2, 0)
    scales = cell_size.reshape(partitions, elem_count)
    sounds = sound_speed.reshape(partitions, elem_count)
    velocity = jnp.moveaxis(vertex_velocity.reshape(3, partitions, OWN_VERTS), 1, 0)
    shares = jnp.moveaxis(share_index.reshape(2, partitions, SHARED_VERTS), 1, 0)
    down_set = jax.vmap(lambda vel_part, index_part: vel_part[:, index_part])(velocity, shares[:, 0])
    up_set = jax.vmap(lambda vel_part, index_part: vel_part[:, index_part])(velocity, shares[:, 1])
    up_grid = up_set.reshape(SLABS, PEERS, 3, SHARED_VERTS)
    down_grid = down_set.reshape(SLABS, PEERS, 3, SHARED_VERTS)
    from_lower = jnp.concatenate([jnp.zeros_like(up_grid[:1]), up_grid[:-1]], axis=0).reshape(partitions, 3, SHARED_VERTS)
    from_upper = jnp.concatenate([down_grid[1:], jnp.zeros_like(down_grid[:1])], axis=0).reshape(partitions, 3, SHARED_VERTS)
    vertex_table = jnp.concatenate([velocity, from_lower, from_upper], axis=2)
    corners = jnp.moveaxis(elem_vertex.reshape(4, partitions, elem_count), 1, 0)
    mesh_all = jax.vmap(lambda tab, cor: (tab[:, cor[0]] + tab[:, cor[1]] + tab[:, cor[2]] + tab[:, cor[3]]) * 0.25)(vertex_table, corners)
    wave_bound = sounds + jnp.abs(mesh_all[:, 0]) + jnp.abs(mesh_all[:, 1]) + jnp.abs(mesh_all[:, 2])
    step_size = CFL_NUMBER * jnp.min(scales / wave_bound)

    slab_e = jnp.moveaxis(slab_elem.reshape(2, partitions, SLAB_FACES), 1, 0).reshape(partitions, 2 * SLAB_FACES)
    slab_f = jnp.moveaxis(slab_face.reshape(2, partitions, SLAB_FACES), 1, 0).reshape(partitions, 2 * SLAB_FACES)
    slab_n = jnp.moveaxis(slab_normal.reshape(3, 2, partitions, SLAB_FACES), 2, 0).reshape(partitions, 3, 2 * SLAB_FACES)
    peer_e = jnp.moveaxis(peer_elem.reshape(PEERS, partitions, PEER_FACES), 1, 0).reshape(partitions, PEERS * PEER_FACES)
    peer_f = jnp.moveaxis(peer_face.reshape(PEERS, partitions, PEER_FACES), 1, 0).reshape(partitions, PEERS * PEER_FACES)
    peer_n = jnp.moveaxis(peer_normal.reshape(3, PEERS, partitions, PEER_FACES), 2, 0).reshape(partitions, 3, PEERS * PEER_FACES)
    peer_c = peer_count.reshape(PEERS, partitions).T
    inner_e = jnp.moveaxis(inner_elem.reshape(2, partitions, INNER_FACES), 1, 0)
    inner_f = jnp.moveaxis(inner_face.reshape(2, partitions, INNER_FACES), 1, 0)
    inner_n = jnp.moveaxis(inner_normal.reshape(3, partitions, INNER_FACES), 1, 0)

    def sends(packed):
        coeffs, cell_scale, mesh_vel, bound_row, s_elem, s_face, p_elem, p_face = packed
        predicted = predict(coeffs, mesh_vel, cell_scale, step_size, jacobian, derivative)
        face_table = all_traces(predicted, restriction)
        return (pick(face_table, bound_row, s_elem, s_face, elem_count), pick(face_table, bound_row, p_elem, p_face, elem_count))

    slab_send, peer_send = lax.map(sends, (states, scales, mesh_all, wave_bound, slab_e, slab_f, peer_e, peer_f))
    trace_rows = num_vars * face_basis + 1
    slab_grid = slab_send.reshape(SLABS, PEERS, trace_rows, 2 * SLAB_FACES)
    low_part = jnp.concatenate([jnp.zeros_like(slab_grid[:1, :, :, SLAB_FACES:]), slab_grid[:-1, :, :, SLAB_FACES:]], axis=0)
    high_part = jnp.concatenate([slab_grid[1:, :, :, :SLAB_FACES], jnp.zeros_like(slab_grid[:1, :, :, :SLAB_FACES])], axis=0)
    slab_recv = jnp.concatenate([low_part, high_part], axis=3).reshape(partitions, trace_rows, 2 * SLAB_FACES)
    peer_grid = peer_send.reshape(SLABS, PEERS, trace_rows, PEERS, PEER_FACES)
    peer_recv = jnp.transpose(peer_grid, (0, 3, 2, 1, 4)).reshape(partitions, trace_rows, PEERS * PEER_FACES)

    def rates(packed):
        (coeffs, cell_scale, mesh_vel, bound_row, s_elem, s_face, s_norm, s_recv,
         p_elem, p_face, p_norm, p_recv, p_cnt, i_elem, i_face, i_norm) = packed
        predicted = predict(coeffs, mesh_vel, cell_scale, step_size, jacobian, derivative)
        face_table = all_traces(predicted, restriction)
        slab_own = pick(face_table, bound_row, s_elem, s_face, elem_count)
        peer_own = pick(face_table, bound_row, p_elem, p_face, elem_count)
        side_zero = pick(face_table, bound_row, i_elem[0], i_face[0], elem_count)
        side_one = pick(face_table, bound_row, i_elem[1], i_face[1], elem_count)
        live_mask = (jnp.arange(PEER_FACES)[None, :] < p_cnt[:, None]).reshape(-1).astype(jnp.float32)
        values = jnp.concatenate([
            riemann(slab_own, s_recv, s_norm, jacobian, face_basis),
            riemann(peer_own, p_recv, p_norm, jacobian, face_basis) * live_mask[None, :],
            riemann(side_zero, side_one, i_norm, jacobian, face_basis),
            riemann(side_one, side_zero, -i_norm, jacobian, face_basis)], axis=1)
        columns = jnp.concatenate([s_face * elem_count + s_elem, p_face * elem_count + p_elem,
                                   i_face[0] * elem_count + i_elem[0], i_face[1] * elem_count + i_elem[1]])
        lifted = face_rate(columns, values, lifting, num_vars, face_basis, elem_count)
        return -(spatial(predicted, mesh_vel, cell_scale, jacobian, derivative) + lifted / cell_scale[None, None, :])

    result = lax.map(rates, (states, scales, mesh_all, wave_bound, slab_e, slab_f, slab_n, slab_recv,
                             peer_e, peer_f, peer_n, peer_recv, peer_c, inner_e, inner_f, inner_n))
    rate = jnp.moveaxis(result, 0, 2).reshape(VARS, BASIS, partitions * elem_count)
    return rate, step_size
```

```python
import functools

import jax
import jax.numpy as jnp
import numpy as np
from jax import lax
from jax.experimental import pallas as pl
from jax.experimental.pallas import tpu as pltpu
from jax.sharding import PartitionSpec as P

HIGHEST_PREC = lax.Precision.HIGHEST
CFL_NUMBER = 0.3
BF16 = jnp.bfloat16
F32 = jnp.float32

VARS = 11
BASIS = 10
FACE = 6
ROWS = 112
TROWS = 72
ELEM_BLOCK = 256
TILE = 256
CHUNK = 512


def expansion_tables():
    rows = np.arange(ROWS)
    outer = np.zeros((ROWS, 16), np.float32)
    inner = np.zeros((ROWS, 16), np.float32)
    live = rows < VARS * BASIS
    outer[rows[live], rows[live] // VARS] = 1.0
    inner[rows[live], rows[live] % VARS] = 1.0
    face_live = (np.arange(TROWS) < VARS * FACE).astype(np.float32)[:, None]
    outer_face = outer[:TROWS] * face_live
    inner_face = inner[:TROWS] * face_live
    outer3 = np.tile(outer.T, (1, 3))
    inner3 = np.tile(inner.T, (1, 3))
    outer_face3 = np.tile(outer_face.T, (1, 3))
    inner_face3 = np.tile(inner_face.T, (1, 3))
    bound = np.zeros((TROWS, 3 * ROWS), np.float32)
    bound[VARS * FACE, VARS * BASIS :: ROWS] = 1.0
    return (outer, inner, outer_face, inner_face, outer3, inner3, outer_face3, inner_face3, bound)


def exact_dot(left, right):
    return jnp.dot(left, right, precision=HIGHEST_PREC, preferred_element_type=F32)


def split3_cols(wide):
    third = wide.shape[1] // 3
    high = wide.astype(BF16).astype(F32)
    lane = lax.broadcasted_iota(jnp.int32, wide.shape, 1)
    return jnp.where(lane < 2 * third, high, wide - high).astype(BF16)


def weights_kernel(
    jac, der, res, lif, outer, inner, outer_face, inner_face, outer3, inner3, outer_face3,
    inner_face3, bound, w_elem, w_trace, w_flux, w_lift,
):
    same_var = exact_dot(inner[...], inner3[...])
    total = None
    for d in range(3):
        der_wide = exact_dot(outer[...], exact_dot(der[d], outer3[...]))
        jac_wide = exact_dot(inner[...], exact_dot(jac[d], inner3[...]))
        term = der_wide * jac_wide
        total = term if total is None else total + term
        w_elem[(d + 1) * ROWS : (d + 2) * ROWS, :] = split3_cols(der_wide * same_var)
        same_basis = exact_dot(outer_face[...], outer_face3[...])
        jac_face = exact_dot(inner_face[...], exact_dot(jac[d], inner_face3[...]))
        w_flux[d * TROWS : (d + 1) * TROWS, :] = split3_cols(jac_face * same_basis)
    w_elem[0:ROWS, :] = split3_cols(total)
    same_var_in = exact_dot(inner_face[...], inner3[...])
    same_var_out = exact_dot(inner[...], inner_face3[...])
    for k in range(4):
        res_wide = exact_dot(outer_face[...], exact_dot(res[k], outer3[...]))
        w_trace[k * TROWS : (k + 1) * TROWS, :] = split3_cols(res_wide * same_var_in + bound[...])
        lif_wide = exact_dot(outer[...], exact_dot(lif[k], outer_face3[...]))
        w_lift[k * ROWS : (k + 1) * ROWS, :] = split3_cols(lif_wide * same_var_out)


def make_weights(jacobian, derivative, restriction, lifting):
    tables = [jnp.asarray(table) for table in expansion_tables()]
    padded = [
        jnp.pad(value, ((0, 0), (0, 16 - value.shape[1]), (0, 16 - value.shape[2])))
        for value in (jacobian, derivative, restriction, lifting)
    ]
    return pl.pallas_call(
        weights_kernel,
        out_shape=(
            jax.ShapeDtypeStruct((4 * ROWS, 3 * ROWS), BF16),
            jax.ShapeDtypeStruct((4 * TROWS, 3 * ROWS), BF16),
            jax.ShapeDtypeStruct((3 * TROWS, 3 * TROWS), BF16),
            jax.ShapeDtypeStruct((4 * ROWS, 3 * TROWS), BF16),
        ),
        name="weights",
    )(*padded, *tables)


def lane_gather(table, tiles, index_row):
    wide = jnp.broadcast_to(index_row, (8, 128))
    low = wide & 127
    high = lax.shift_right_logical(wide, 7)
    picked = jnp.take_along_axis(table[:, 0:128], low, axis=1)
    for t in range(1, tiles):
        other = jnp.take_along_axis(table[:, t * 128 : (t + 1) * 128], low, axis=1)
        picked = jnp.where(high == t, other, picked)
    return picked


def share_kernel(velocity, share, to_lower, to_upper, table):
    table[...] = jnp.zeros_like(table)
    table[0:3, :] = velocity[...]
    tiles = velocity.shape[1] // 128
    to_lower[...] = lane_gather(table, tiles, share[0:1, :])
    to_upper[...] = lane_gather(table, tiles, share[1:2, :])


def mesh_kernel(velocity, from_lower, from_upper, corners, sizes, sounds, geom, least, table):
    own = velocity.shape[1]
    table[...] = jnp.zeros_like(table)
    table[0:3, 0:own] = velocity[...]
    table[:, own : own + 128] = from_lower[...]
    table[:, own + 128 : own + 256] = from_upper[...]
    tiles = (own + 256) // 128
    elems = corners.shape[1]
    for j in range(elems // 128):
        cols = slice(j * 128, (j + 1) * 128)
        total = None
        for corner in range(4):
            value = lane_gather(table, tiles, corners[corner : corner + 1, cols])
            total = value if total is None else total + value
        geom[:, cols] = total * 0.25
    moves = jnp.abs(geom[0:3, :])
    bound = sounds[...] + moves[0:1] + moves[1:2] + moves[2:3]
    geom[3:4, :] = bound
    geom[4:5, :] = 1.0 / sizes[...]
    least[...] = jnp.broadcast_to(
        jnp.min(sizes[...] / bound, axis=1, keepdims=True), least.shape
    )


def split3_rows(value):
    high = value.astype(BF16)
    low = (value - high.astype(F32)).astype(BF16)
    return jnp.concatenate([high, low, high], axis=0)


def split2_rows(value):
    high = value.astype(BF16)
    low = (value - high.astype(F32)).astype(BF16)
    return jnp.concatenate([high, low], axis=0)


def fields_kernel(state, geom, w_elem, c_out, l1_out, l2_out, l3_out, table):
    for b in range(BASIS):
        c_out[b * VARS : (b + 1) * VARS, :] = state[b]
    c_out[BASIS * VARS : BASIS * VARS + 1, :] = geom[3:4, :]
    c_out[BASIS * VARS + 1 : ROWS, :] = jnp.zeros((1, c_out.shape[1]), F32)
    value = c_out[...]
    for i, out in enumerate((l1_out, l2_out, l3_out)):
        pieces = split3_rows(value)
        table[2 * ROWS * i : 2 * ROWS * (i + 1), :] = pieces[0 : 2 * ROWS]
        parts = jnp.dot(w_elem[...], pieces, preferred_element_type=F32)
        value = (
            parts[0:ROWS]
            - geom[0:1, :] * parts[ROWS : 2 * ROWS]
            - geom[1:2, :] * parts[2 * ROWS : 3 * ROWS]
            - geom[2:3, :] * parts[3 * ROWS : 4 * ROWS]
        ) * geom[4:5, :]
        out[...] = value


def make_fields(state, geom, w_elem):
    elems = geom.shape[1]
    full = jax.ShapeDtypeStruct((ROWS, elems), F32)
    block = pl.BlockSpec((ROWS, CHUNK), lambda i: (0, i))
    return pl.pallas_call(
        fields_kernel,
        grid=(elems // CHUNK,),
        in_specs=[
            pl.BlockSpec((BASIS, VARS, CHUNK), lambda i: (0, 0, i)),
            pl.BlockSpec((8, CHUNK), lambda i: (0, i)),
            pl.BlockSpec((4 * ROWS, 3 * ROWS), lambda i: (0, 0)),
        ],
        out_specs=[block] * 4 + [pl.BlockSpec((6 * ROWS, CHUNK), lambda i: (0, i))],
        out_shape=[full] * 4 + [jax.ShapeDtypeStruct((6 * ROWS, elems), BF16)],
        name="fields",
    )(state, geom, w_elem)


def build_selection(index_row, select):
    count = index_row.shape[1]
    low = index_row & (ELEM_BLOCK - 1)
    high = lax.shift_right_logical(index_row, 8)
    place = lax.broadcasted_iota(jnp.int32, (ELEM_BLOCK, count), 0)
    match = jnp.where(place == low, 1.0, 0.0).astype(BF16)
    for t in range(select.shape[0] // ELEM_BLOCK):
        here = jnp.where(high == t, 1.0, 0.0).astype(BF16)
        select[t * ELEM_BLOCK : (t + 1) * ELEM_BLOCK, :] = match * here


def choose(stacked, which, rows):
    value = stacked[0:rows]
    for k in range(1, 4):
        value = jnp.where(which == k, stacked[k * rows : (k + 1) * rows], value)
    return value


def traces_of(picked, which, w_trace):
    pieces = jnp.concatenate([picked, picked[0:ROWS]], axis=0)
    stacked = jnp.dot(w_trace[...], pieces, preferred_element_type=F32)
    return choose(stacked, which, TROWS)


def border_kernel(elem, face, table, w_trace, own, to_lower, to_upper, to_peer, select):
    step = pl.program_id(0)
    build_selection(elem[...], select)
    picked = jnp.dot(table[...], select[...], preferred_element_type=F32).astype(BF16)
    which = face[...]
    own[3 * TROWS :, :] = jnp.zeros((8, own.shape[1]), F32)
    for i in range(3):
        own[i * TROWS : (i + 1) * TROWS, :] = traces_of(
            picked[2 * ROWS * i : 2 * ROWS * (i + 1)], which, w_trace
        )

    @pl.when(step == 0)
    def _():
        to_lower[...] = own[0 : 3 * TROWS, 0:256]
        to_upper[...] = own[0 : 3 * TROWS, 256:512]

    @pl.when(step == 1)
    def _():
        left = lax.broadcasted_iota(jnp.int32, (ROWS, 128), 1) < 64
        for m in range(4):
            top = own[0:ROWS, m * 128 : (m + 1) * 128]
            bottom = own[ROWS : 2 * ROWS, m * 128 : (m + 1) * 128]
            to_peer[2 * m] = jnp.where(left, top, pltpu.roll(bottom, 64, 1))
            to_peer[2 * m + 1] = jnp.where(left, pltpu.roll(top, 64, 1), bottom)


def make_border(elem, face, table, w_trace):
    elems = table.shape[1]
    return pl.pallas_call(
        border_kernel,
        grid=(2,),
        in_specs=[
            pl.BlockSpec((1, 512), lambda i: (0, i)),
            pl.BlockSpec((1, 512), lambda i: (0, i)),
            pl.BlockSpec((6 * ROWS, elems), lambda i: (0, 0)),
            pl.BlockSpec((4 * TROWS, 3 * ROWS), lambda i: (0, 0)),
        ],
        out_specs=[
            pl.BlockSpec((2 * ROWS, 512), lambda i: (0, i)),
            pl.BlockSpec((3 * TROWS, 256), lambda i: (0, 0)),
            pl.BlockSpec((3 * TROWS, 256), lambda i: (0, 0)),
            pl.BlockSpec((8, ROWS, 128), lambda i: (0, 0, 0)),
        ],
        out_shape=[
            jax.ShapeDtypeStruct((2 * ROWS, 1024), F32),
            jax.ShapeDtypeStruct((3 * TROWS, 256), F32),
            jax.ShapeDtypeStruct((3 * TROWS, 256), F32),
            jax.ShapeDtypeStruct((8, ROWS, 128), F32),
        ],
        scratch_shapes=[pltpu.VMEM((elems, 512), BF16)],
        name="border",
    )(elem, face, table, w_trace)


def flux_parts(own, theirs, normal, w_flux):
    jump = theirs - own
    bound = jnp.maximum(own[66:67], theirs[66:67])
    parts = jnp.dot(w_flux[...], split3_rows(jump), preferred_element_type=F32)
    central = (
        normal[0:1] * parts[0:TROWS]
        + normal[1:2] * parts[TROWS : 2 * TROWS]
        + normal[2:3] * parts[2 * TROWS : 3 * TROWS]
    )
    return central, bound * jump


def lift_and_add(values, which, w_lift, select, total):
    stacked = jnp.dot(w_lift[...], split3_rows(values), preferred_element_type=F32)
    pieces = split2_rows(choose(stacked, which, ROWS))
    total[...] += lax.dot_general(
        pieces, select[...], (((1,), (1,)), ((), ())), preferred_element_type=F32
    )


def combine(first, second, third, half, sixth):
    return first + half * second + sixth * third


def rate_kernel(
    step_ref, c_ref, l1_ref, l2_ref, l3_ref, geom, own, from_lower, from_upper, from_peer, b_elem,
    b_face, b_normal, b_live, elem, face, normal, w_trace, w_flux, w_lift, out, table, total,
    select, theirs,
):
    step = pl.program_id(0)
    tau = step_ref[0, 0]
    half = -0.5 * tau
    sixth = tau * tau / 6.0

    @pl.when(step == 0)
    def _():
        total[...] = jnp.zeros_like(total)
        for j in range(c_ref.shape[1] // CHUNK):
            cols = slice(j * CHUNK, (j + 1) * CHUNK)
            table[:, cols] = split2_rows(
                combine(c_ref[:, cols], l1_ref[:, cols], l2_ref[:, cols], half, sixth)
            )
        left = lax.broadcasted_iota(jnp.int32, (ROWS, 128), 1) < 64
        theirs[0 : 3 * TROWS, 0:256] = from_lower[...]
        theirs[0 : 3 * TROWS, 256:512] = from_upper[...]
        for m in range(4):
            cols = slice(512 + m * 128, 512 + (m + 1) * 128)
            one, two = from_peer[2 * m], from_peer[2 * m + 1]
            theirs[0:ROWS, cols] = jnp.where(left, one, pltpu.roll(two, 64, 1))
            theirs[ROWS : 2 * ROWS, cols] = jnp.where(left, pltpu.roll(one, 64, 1), two)
        for j in range(2):
            cols = slice(j * 512, (j + 1) * 512)
            build_selection(b_elem[:, cols], select)

            def merged(ref):
                return combine(
                    ref[0:TROWS, cols],
                    ref[TROWS : 2 * TROWS, cols],
                    ref[2 * TROWS : 3 * TROWS, cols],
                    half,
                    sixth,
                )

            central, upwind = flux_parts(merged(own), merged(theirs), b_normal[:, cols], w_flux)
            values = (0.5 * (central - upwind)) * b_live[:, cols]
            lift_and_add(values, b_face[:, cols], w_lift, select, total)

    index_row = jnp.concatenate([elem[0:1, :], elem[1:2, :]], axis=1)
    which = jnp.concatenate([face[0:1, :], face[1:2, :]], axis=1)
    build_selection(index_row, select)
    picked = jnp.dot(table[...], select[...], preferred_element_type=F32).astype(BF16)
    traces = traces_of(picked, which, w_trace)
    central, upwind = flux_parts(traces[:, 0:TILE], traces[:, TILE:], normal[...], w_flux)
    values = jnp.concatenate([0.5 * (central - upwind), 0.5 * (central + upwind)], axis=1)
    lift_and_add(values, which, w_lift, select, total)

    @pl.when(step == pl.num_programs(0) - 1)
    def _():
        for j in range(c_ref.shape[1] // CHUNK):
            cols = slice(j * CHUNK, (j + 1) * CHUNK)
            lifted = total[0:ROWS, cols] + total[ROWS : 2 * ROWS, cols]
            volume = combine(l1_ref[:, cols], l2_ref[:, cols], l3_ref[:, cols], half, sixth)
            rate = -(volume + lifted * geom[4:5, cols])
            for b in range(BASIS):
                out[b, :, cols] = rate[b * VARS : (b + 1) * VARS]


def make_rate(step_size, fields, geom, own, received, border, inner, weights):
    elems = geom.shape[1]
    faces = inner[0].shape[1]
    whole = pl.BlockSpec(memory_space=pltpu.VMEM)
    tiled = lambda rows: pl.BlockSpec((rows, TILE), lambda i: (0, i))
    return pl.pallas_call(
        rate_kernel,
        grid=(faces // TILE,),
        in_specs=[pl.BlockSpec(memory_space=pltpu.SMEM)]
        + [whole] * 13
        + [tiled(2), tiled(2), tiled(3)]
        + [whole] * 3,
        out_specs=whole,
        out_shape=jax.ShapeDtypeStruct((BASIS, VARS, elems), F32),
        scratch_shapes=[
            pltpu.VMEM((2 * ROWS, elems), BF16),
            pltpu.VMEM((2 * ROWS, elems), F32),
            pltpu.VMEM((elems, 2 * TILE), BF16),
            pltpu.VMEM((2 * ROWS, 1024), F32),
        ],
        name="rate",
    )(step_size, *fields, geom, own, *received, *border, *inner, *weights)


def body(
    conserved,
    cell_size,
    sound_speed,
    jacobian,
    derivative,
    restriction,
    lifting,
    vertex_velocity,
    share_index,
    elem_vertex,
    inner_elem,
    inner_face,
    inner_normal,
    slab_elem,
    slab_face,
    slab_normal,
    peer_elem,
    peer_face,
    peer_normal,
    peer_count,
):
    elems = conserved.shape[2]
    slabs = lax.axis_size("shock")
    devices = slabs * lax.axis_size("trans")
    up = [(i, i + 1) for i in range(slabs - 1)]
    down = [(i + 1, i) for i in range(slabs - 1)]

    shared = jax.ShapeDtypeStruct((8, 128), F32)
    to_lower, to_upper = pl.pallas_call(
        share_kernel,
        out_shape=(shared, shared),
        scratch_shapes=[pltpu.VMEM((8, vertex_velocity.shape[1]), F32)],
        name="share",
    )(vertex_velocity, share_index)
    from_lower = lax.ppermute(to_upper, "shock", up)
    from_upper = lax.ppermute(to_lower, "shock", down)
    w_elem, w_trace, w_flux, w_lift = make_weights(jacobian, derivative, restriction, lifting)
    geom, least = pl.pallas_call(
        mesh_kernel,
        out_shape=(
            jax.ShapeDtypeStruct((8, elems), F32),
            jax.ShapeDtypeStruct((1, devices), F32),
        ),
        scratch_shapes=[pltpu.VMEM((8, vertex_velocity.shape[1] + 256), F32)],
        name="mesh",
    )(
        vertex_velocity,
        from_lower,
        from_upper,
        elem_vertex,
        cell_size.reshape(1, elems),
        sound_speed.reshape(1, elems),
    )
    all_least = lax.all_to_all(
        least.reshape(devices), ("shock", "trans"), split_axis=0, concat_axis=0, tiled=True
    )

    state = jnp.transpose(conserved, (1, 0, 2))
    *fields, table = make_fields(state, geom, w_elem)
    live = (jnp.arange(peer_elem.shape[1])[None, :] < peer_count).astype(F32)
    b_elem = jnp.concatenate([slab_elem.reshape(1, -1), peer_elem.reshape(1, -1)], axis=1)
    b_face = jnp.concatenate([slab_face.reshape(1, -1), peer_face.reshape(1, -1)], axis=1)
    b_normal = jnp.concatenate([slab_normal.reshape(3, -1), peer_normal.reshape(3, -1)], axis=1)
    b_live = jnp.concatenate([jnp.ones((1, slab_elem.size), F32), live.reshape(1, -1)], axis=1)
    own, slab_down, slab_up, peer_send = make_border(b_elem, b_face, table, w_trace)
    slab_lower = lax.ppermute(slab_up, "shock", up)
    slab_upper = lax.ppermute(slab_down, "shock", down)
    peer_recv = lax.all_to_all(peer_send, "trans", split_axis=0, concat_axis=0, tiled=True)

    step_size = CFL_NUMBER * jnp.min(all_least)
    rate = make_rate(
        step_size.reshape(1, 1),
        fields,
        geom,
        own,
        (slab_lower, slab_upper, peer_recv),
        (b_elem, b_face, b_normal, b_live),
        (inner_elem, inner_face, inner_normal),
        (w_trace, w_flux, w_lift),
    )
    return (jnp.transpose(rate, (1, 0, 2)), step_size)


def solution(mesh):
    return jax.shard_map(
        body,
        mesh=mesh,
        in_specs=(
            P(None, None, ("shock", "trans")),
            P(("shock", "trans")),
            P(("shock", "trans")),
            P(),
            P(),
            P(),
            P(),
            P(None, ("shock", "trans")),
            P(None, ("shock", "trans")),
            P(None, ("shock", "trans")),
            P(None, ("shock", "trans")),
            P(None, ("shock", "trans")),
            P(None, ("shock", "trans")),
            P(None, ("shock", "trans")),
            P(None, ("shock", "trans")),
            P(None, None, ("shock", "trans")),
            P(None, ("shock", "trans")),
            P(None, ("shock", "trans")),
            P(None, None, ("shock", "trans")),
            P(None, ("shock", "trans")),
        ),
        out_specs=(P(None, None, ("shock", "trans")), P()),
        check_vma=False,
    )
```

```python
import functools

import jax
import jax.numpy as jnp
import numpy as np
from jax import lax
from jax.experimental import pallas as pl
from jax.experimental.pallas import tpu as pltpu
from jax.sharding import PartitionSpec as P

HIGHEST_PREC = lax.Precision.HIGHEST
CFL_NUMBER = 0.3
BF16 = jnp.bfloat16
F32 = jnp.float32

VARS = 11
BASIS = 10
FACE = 6
ROWS = 112
TROWS = 72
ELEM_BLOCK = 256
TILE = 512
CHUNK = 512


def expansion_tables():
    rows = np.arange(ROWS)
    outer = np.zeros((ROWS, 16), np.float32)
    inner = np.zeros((ROWS, 16), np.float32)
    live = rows < VARS * BASIS
    outer[rows[live], rows[live] // VARS] = 1.0
    inner[rows[live], rows[live] % VARS] = 1.0
    face_live = (np.arange(TROWS) < VARS * FACE).astype(np.float32)[:, None]
    outer_face = outer[:TROWS] * face_live
    inner_face = inner[:TROWS] * face_live
    thrice = lambda matrix: np.tile(matrix, (1, 3))
    bound = np.zeros((TROWS, ROWS), np.float32)
    bound[VARS * FACE, VARS * BASIS] = 1.0
    return (
        thrice(outer.T),
        thrice(inner.T),
        thrice(outer_face.T),
        thrice(inner_face.T),
        thrice(inner @ inner.T),
        thrice(inner_face @ inner.T),
        thrice(inner @ inner_face.T),
        thrice(outer_face @ outer_face.T),
        thrice(bound),
    )


def exact_dot(left, right, contract=((1,), (0,))):
    return lax.dot_general(
        left, right, (contract, ((), ())), precision=HIGHEST_PREC, preferred_element_type=F32
    )


def split3_cols(wide):
    third = wide.shape[1] // 3
    high = wide.astype(BF16).astype(F32)
    lane = lax.broadcasted_iota(jnp.int32, wide.shape, 1)
    return jnp.where(lane < 2 * third, high, wide - high).astype(BF16)


def weights_kernel(
    jac, der, res, lif, outer3, inner3, outer_face3, inner_face3, var_elem, var_trace, var_lift,
    basis_face, bound, w_elem, w_trace, w_flux, w_lift, small, wide_a, wide_b, face_a,
):
    small[...] = jnp.zeros_like(small)
    wide_a[...] = jnp.zeros_like(wide_a)
    wide_b[...] = jnp.zeros_like(wide_b)
    face_a[...] = jnp.zeros_like(face_a)
    for d in range(3):
        small[16 * d : 16 * d + VARS, 0:VARS] = jac[:, d, :]
        small[48 + 16 * d : 48 + 16 * d + BASIS, 0:BASIS] = der[:, d, :]
    for k in range(4):
        small[96 + 16 * k : 96 + 16 * k + FACE, 0:BASIS] = res[:, k, :]
        small[160 + 16 * k : 160 + 16 * k + FACE, 0:BASIS] = lif[:, k, :]
    jac_cols = exact_dot(small[0:48, :], inner3[...])
    jac_face_cols = exact_dot(small[0:48, :], inner_face3[...])
    other_cols = exact_dot(small[48:160, :], outer3[...])

    def repeat_rows(cols, first, target, count):
        for b in range(count):
            target[b * VARS : (b + 1) * VARS, :] = jnp.broadcast_to(
                cols[first + b : first + b + 1], (VARS, cols.shape[1])
            )

    def tile_rows(cols, first, target, count):
        for b in range(count):
            target[b * VARS : (b + 1) * VARS, :] = cols[first : first + VARS]

    total = None
    for d in range(3):
        repeat_rows(other_cols, 16 * d, wide_a, BASIS)
        tile_rows(jac_cols, 16 * d, wide_b, BASIS)
        term = wide_a[...] * wide_b[...]
        total = term if total is None else total + term
        w_elem[(d + 1) * ROWS : (d + 2) * ROWS, :] = split3_cols(wide_a[...] * var_elem[...])
        tile_rows(jac_face_cols, 16 * d, face_a, FACE)
        w_flux[d * TROWS : (d + 1) * TROWS, :] = split3_cols(face_a[0:TROWS] * basis_face[...])
    w_elem[0:ROWS, :] = split3_cols(total)
    for k in range(4):
        repeat_rows(other_cols, 48 + 16 * k, wide_a, FACE)
        w_trace[k * TROWS : (k + 1) * TROWS, :] = split3_cols(
            wide_a[0:TROWS] * var_trace[...] + bound[...]
        )
        lif_cols = exact_dot(
            small[160 + 16 * k : 176 + 16 * k, :], outer_face3[...], ((0,), (0,))
        )
        repeat_rows(lif_cols, 0, face_a, BASIS)
        w_lift[k * ROWS : (k + 1) * ROWS, :] = split3_cols(face_a[...] * var_lift[...])


def make_weights(jacobian, derivative, restriction, lifting):
    tables = [jnp.asarray(table) for table in expansion_tables()]
    return pl.pallas_call(
        weights_kernel,
        out_shape=(
            jax.ShapeDtypeStruct((4 * ROWS, 3 * ROWS), BF16),
            jax.ShapeDtypeStruct((4 * TROWS, 3 * ROWS), BF16),
            jax.ShapeDtypeStruct((3 * TROWS, 3 * TROWS), BF16),
            jax.ShapeDtypeStruct((4 * ROWS, 3 * TROWS), BF16),
        ),
        scratch_shapes=[
            pltpu.VMEM((224, 16), F32),
            pltpu.VMEM((ROWS, 3 * ROWS), F32),
            pltpu.VMEM((ROWS, 3 * ROWS), F32),
            pltpu.VMEM((ROWS, 3 * TROWS), F32),
        ],
        cost_estimate=pl.CostEstimate(flops=4_000_000, bytes_accessed=2_000_000, transcendentals=0),
        name="weights",
    )(
        jnp.transpose(jacobian, (1, 0, 2)),
        jnp.transpose(derivative, (1, 0, 2)),
        jnp.transpose(restriction, (1, 0, 2)),
        jnp.transpose(lifting, (2, 0, 1)),
        *tables,
    )


def lane_gather(table, tiles, index_row):
    wide = jnp.broadcast_to(index_row, (8, 128))
    low = wide & 127
    high = lax.shift_right_logical(wide, 7)
    picked = jnp.take_along_axis(table[:, 0:128], low, axis=1)
    for t in range(1, tiles):
        other = jnp.take_along_axis(table[:, t * 128 : (t + 1) * 128], low, axis=1)
        picked = jnp.where(high == t, other, picked)
    return picked


def share_kernel(velocity, share, to_lower, to_upper, table):
    table[...] = jnp.zeros_like(table)
    table[0:3, :] = velocity[...]
    tiles = velocity.shape[1] // 128
    to_lower[...] = lane_gather(table, tiles, share[0:1, :])
    to_upper[...] = lane_gather(table, tiles, share[1:2, :])


def mesh_kernel(velocity, from_lower, from_upper, corners, sizes, sounds, geom, least, table):
    own = velocity.shape[1]
    table[...] = jnp.zeros_like(table)
    table[0:3, 0:own] = velocity[...]
    table[:, own : own + 128] = from_lower[...]
    table[:, own + 128 : own + 256] = from_upper[...]
    tiles = (own + 256) // 128
    elems = corners.shape[1]
    for j in range(elems // 128):
        cols = slice(j * 128, (j + 1) * 128)
        total = None
        for corner in range(4):
            value = lane_gather(table, tiles, corners[corner : corner + 1, cols])
            total = value if total is None else total + value
        geom[:, cols] = total * 0.25
    moves = jnp.abs(geom[0:3, :])
    bound = sounds[...] + moves[0:1] + moves[1:2] + moves[2:3]
    geom[3:4, :] = bound
    geom[4:5, :] = 1.0 / sizes[...]
    least[...] = jnp.broadcast_to(
        jnp.min(sizes[...] / bound, axis=1, keepdims=True)[None], least.shape
    )


def split3_rows(value):
    high = value.astype(BF16)
    low = (value - high.astype(F32)).astype(BF16)
    return jnp.concatenate([high, low, high], axis=0)


def split2_rows(value):
    high = value.astype(BF16)
    low = (value - high.astype(F32)).astype(BF16)
    return jnp.concatenate([high, low], axis=0)


def apply_operator(pieces, geom, w_elem, cols):
    parts = jnp.dot(w_elem[...], pieces, preferred_element_type=F32)
    return (
        parts[0:ROWS]
        - geom[0:1, cols] * parts[ROWS : 2 * ROWS]
        - geom[1:2, cols] * parts[2 * ROWS : 3 * ROWS]
        - geom[2:3, cols] * parts[3 * ROWS : 4 * ROWS]
    ) * geom[4:5, cols]


def third_kernel(l2_ref, geom, w_elem, l3_out):
    l3_out[...] = apply_operator(split3_rows(l2_ref[...]), geom, w_elem, slice(None))


def make_third(second, geom, w_elem):
    elems = geom.shape[1]
    return pl.pallas_call(
        third_kernel,
        grid=(elems // CHUNK,),
        in_specs=[
            pl.BlockSpec((ROWS, CHUNK), lambda i: (0, i)),
            pl.BlockSpec((8, CHUNK), lambda i: (0, i)),
            pl.BlockSpec((4 * ROWS, 3 * ROWS), lambda i: (0, 0)),
        ],
        out_specs=pl.BlockSpec((ROWS, CHUNK), lambda i: (0, i)),
        out_shape=jax.ShapeDtypeStruct((ROWS, elems), F32),
        cost_estimate=pl.CostEstimate(
            flops=2 * 448 * 336 * elems, bytes_accessed=2_000_000, transcendentals=0
        ),
        name="third",
    )(second, geom, w_elem)


def build_selection(index_row, select):
    count = index_row.shape[1]
    low = index_row & (ELEM_BLOCK - 1)
    high = lax.shift_right_logical(index_row, 8)
    place = lax.broadcasted_iota(jnp.int32, (ELEM_BLOCK, count), 0)
    match = jnp.where(place == low, 1.0, 0.0).astype(BF16)
    for t in range(select.shape[0] // ELEM_BLOCK):
        here = jnp.where(high == t, 1.0, 0.0).astype(BF16)
        select[t * ELEM_BLOCK : (t + 1) * ELEM_BLOCK, :] = match * here


def choose(stacked, which, rows):
    value = stacked[0:rows]
    for k in range(1, 4):
        value = jnp.where(which == k, stacked[k * rows : (k + 1) * rows], value)
    return value


def traces_of(picked, which, w_trace):
    pieces = jnp.concatenate([picked, picked[0:ROWS]], axis=0)
    stacked = jnp.dot(w_trace[...], pieces, preferred_element_type=F32)
    return choose(stacked, which, TROWS)


def join_slab(ref):
    return jnp.concatenate([ref[0:1, :], ref[1:2, :]], axis=1)


def join_peers(value):
    wide = jnp.concatenate([value, value], axis=1)
    left = lax.broadcasted_iota(jnp.int32, (1, 128), 1) < 64
    return jnp.concatenate(
        [
            jnp.where(left, wide[2 * m : 2 * m + 1], wide[2 * m + 1 : 2 * m + 2])
            for m in range(4)
        ],
        axis=1,
    )


def front_kernel(
    state, geom, least, s_elem, s_face, p_elem, p_face, w_elem, w_trace, c_out, l1_out, l2_out,
    own, to_lower, to_upper, to_peer, table, select,
):
    step = pl.program_id(0)
    chunks = table.shape[1] // CHUNK

    @pl.when(step < chunks)
    def _():
        cols = pl.ds(pl.multiple_of(step * CHUNK, CHUNK), CHUNK)
        for b in range(BASIS):
            c_out[b * VARS : (b + 1) * VARS, :] = state[b]
        c_out[BASIS * VARS : BASIS * VARS + 1, :] = geom[3:4, cols]
        c_out[BASIS * VARS + 1 : ROWS, :] = jnp.zeros((1, CHUNK), F32)
        pieces = split3_rows(c_out[...])
        table[0 : 2 * ROWS, cols] = pieces[0 : 2 * ROWS]
        l1_out[...] = apply_operator(pieces, geom, w_elem, cols)
        pieces = split3_rows(l1_out[...])
        table[2 * ROWS : 4 * ROWS, cols] = pieces[0 : 2 * ROWS]
        l2_out[...] = apply_operator(pieces, geom, w_elem, cols)
        table[4 * ROWS : 6 * ROWS, cols] = split2_rows(l2_out[...])

    def border(index_row, which):
        build_selection(index_row, select)
        picked = jnp.dot(table[...], select[...], preferred_element_type=F32).astype(BF16)
        own[3 * TROWS :, :] = jnp.zeros((8, own.shape[1]), F32)
        for i in range(3):
            own[i * TROWS : (i + 1) * TROWS, :] = traces_of(
                picked[2 * ROWS * i : 2 * ROWS * (i + 1)], which, w_trace
            )

    @pl.when(step == chunks)
    def _():
        border(join_slab(s_elem), join_slab(s_face))
        to_lower[...] = own[0 : 3 * TROWS, 0:256]
        to_upper[...] = own[0 : 3 * TROWS, 256:512]

    @pl.when(step == chunks + 1)
    def _():
        border(join_peers(p_elem[...]), join_peers(p_face[...]))
        lane = lax.broadcasted_iota(jnp.int32, (ROWS, 128), 1)
        left = lane < 64
        spare = (lax.broadcasted_iota(jnp.int32, (ROWS, 128), 0) == ROWS - 1) & (lane >= 64)
        smallest = jnp.min(least[...])
        for m in range(4):
            top = own[0:ROWS, m * 128 : (m + 1) * 128]
            bottom = own[ROWS : 2 * ROWS, m * 128 : (m + 1) * 128]
            one = jnp.where(left, top, pltpu.roll(bottom, 64, 1))
            two = jnp.where(left, pltpu.roll(top, 64, 1), bottom)
            to_peer[2 * m] = jnp.where(spare, smallest, one)
            to_peer[2 * m + 1] = jnp.where(spare, smallest, two)


def make_front(state, geom, least, border_index, w_elem, w_trace):
    elems = geom.shape[1]
    chunks = elems // CHUNK
    full = jax.ShapeDtypeStruct((ROWS, elems), F32)
    block = pl.BlockSpec((ROWS, CHUNK), lambda i: (0, jnp.minimum(i, chunks - 1)))
    whole = pl.BlockSpec(memory_space=pltpu.VMEM)
    return pl.pallas_call(
        front_kernel,
        grid=(chunks + 2,),
        in_specs=[pl.BlockSpec((BASIS, VARS, CHUNK), lambda i: (0, 0, jnp.minimum(i, chunks - 1)))]
        + [whole] * 8,
        out_specs=[
            block,
            block,
            block,
            pl.BlockSpec((2 * ROWS, 512), lambda i: (0, jnp.maximum(i - chunks, 0))),
            whole,
            whole,
            whole,
        ],
        out_shape=[full] * 3
        + [
            jax.ShapeDtypeStruct((2 * ROWS, 1024), F32),
            jax.ShapeDtypeStruct((3 * TROWS, 256), F32),
            jax.ShapeDtypeStruct((3 * TROWS, 256), F32),
            jax.ShapeDtypeStruct((8, ROWS, 128), F32),
        ],
        scratch_shapes=[pltpu.VMEM((6 * ROWS, elems), BF16), pltpu.VMEM((elems, 512), BF16)],
        name="front",
    )(state, geom, least, *border_index, w_elem, w_trace)


def flux_parts(own, theirs, normal, w_flux):
    jump = theirs - own
    bound = jnp.maximum(own[66:67], theirs[66:67])
    parts = jnp.dot(w_flux[...], split3_rows(jump), preferred_element_type=F32)
    central = (
        normal[0:1] * parts[0:TROWS]
        + normal[1:2] * parts[TROWS : 2 * TROWS]
        + normal[2:3] * parts[2 * TROWS : 3 * TROWS]
    )
    return central, bound * jump


def lift_values(values, which, w_lift):
    stacked = jnp.dot(w_lift[...], split3_rows(values), preferred_element_type=F32)
    return split2_rows(choose(stacked, which, ROWS))


def add_selected(pieces, select, total):
    total[...] += lax.dot_general(
        pieces, select[...], (((1,), (1,)), ((), ())), preferred_element_type=F32
    )


def combine(first, second, third, half, sixth):
    return first + half * second + sixth * third


def rate_kernel(
    c_ref, l1_ref, l2_ref, l3_ref, geom, own, from_lower, from_upper, from_peer, s_elem, s_face,
    s_normal, p_elem, p_face, p_normal, p_count, elem, face, normal, w_trace, w_flux, w_lift, out,
    step_out, table, total, even, odd, theirs, lifted,
):
    step = pl.program_id(0)
    last_tile = elem.shape[1] // TILE - 1
    tau = CFL_NUMBER * jnp.min(from_peer[:, ROWS - 1 : ROWS, 64:128])
    half = -0.5 * tau
    sixth = tau * tau / 6.0

    def sides(tile):
        cols = pl.ds(pl.multiple_of(tile * TILE, TILE), TILE)
        index_row = jnp.concatenate([elem[0:1, cols], elem[1:2, cols]], axis=1)
        which = jnp.concatenate([face[0:1, cols], face[1:2, cols]], axis=1)
        return index_row, which

    def inner_values(tile, traces):
        cols = pl.ds(pl.multiple_of(tile * TILE, TILE), TILE)
        central, upwind = flux_parts(traces[:, 0:TILE], traces[:, TILE:], normal[:, cols], w_flux)
        return jnp.concatenate([0.5 * (central - upwind), 0.5 * (central + upwind)], axis=1)

    @pl.when(step == 0)
    def _():
        step_out[0, 0] = tau
        total[...] = jnp.zeros_like(total)
        for j in range(c_ref.shape[1] // CHUNK):
            cols = slice(j * CHUNK, (j + 1) * CHUNK)
            table[:, cols] = split2_rows(
                combine(c_ref[:, cols], l1_ref[:, cols], l2_ref[:, cols], half, sixth)
            )
        left = lax.broadcasted_iota(jnp.int32, (ROWS, 128), 1) < 64
        theirs[0 : 3 * TROWS, 0:256] = from_lower[...]
        theirs[0 : 3 * TROWS, 256:512] = from_upper[...]
        for m in range(4):
            cols = slice(512 + m * 128, 512 + (m + 1) * 128)
            one, two = from_peer[2 * m], from_peer[2 * m + 1]
            theirs[0:ROWS, cols] = jnp.where(left, one, pltpu.roll(two, 64, 1))
            theirs[ROWS : 2 * ROWS, cols] = jnp.where(left, pltpu.roll(one, 64, 1), two)
        slots = lax.broadcasted_iota(jnp.int32, p_elem.shape, 1)
        alive = jnp.where(slots < p_count[...], 1.0, 0.0)
        b_elem = jnp.concatenate([join_slab(s_elem), join_peers(p_elem[...])], axis=1)
        b_face = jnp.concatenate([join_slab(s_face), join_peers(p_face[...])], axis=1)
        b_live = jnp.concatenate([jnp.ones((1, 512), F32), join_peers(alive)], axis=1)
        b_normal = jnp.concatenate(
            [
                jnp.concatenate([join_slab(s_normal.at[d]), join_peers(p_normal[d])], axis=1)
                for d in range(3)
            ],
            axis=0,
        )
        build_selection(b_elem, odd)
        index_row, _ = sides(0)
        build_selection(index_row, even)

        def merged(ref):
            return combine(
                ref[0:TROWS], ref[TROWS : 2 * TROWS], ref[2 * TROWS : 3 * TROWS], half, sixth
            )

        central, upwind = flux_parts(merged(own), merged(theirs), b_normal, w_flux)
        values = (0.5 * (central - upwind)) * b_live
        lifted[...] = lift_values(values, b_face, w_lift)
        add_selected(lifted[...], odd, total)
    for parity in range(2):
        tile = 2 * step + parity
        cur, nxt = (even, odd) if parity == 0 else (odd, even)
        picked = jnp.dot(table[...], cur[...], preferred_element_type=F32).astype(BF16)
        index_next, _ = sides(jnp.minimum(tile + 1, last_tile))
        build_selection(index_next, nxt)
        _, which = sides(tile)
        values = inner_values(tile, traces_of(picked, which, w_trace))
        add_selected(lift_values(values, which, w_lift), cur, total)
    @pl.when(step == pl.num_programs(0) - 1)
    def _():
        for j in range(c_ref.shape[1] // CHUNK):
            cols = slice(j * CHUNK, (j + 1) * CHUNK)
            summed = total[0:ROWS, cols] + total[ROWS : 2 * ROWS, cols]
            volume = combine(l1_ref[:, cols], l2_ref[:, cols], l3_ref[:, cols], half, sixth)
            rate = -(volume + summed * geom[4:5, cols])
            for b in range(BASIS):
                out[b, :, cols] = rate[b * VARS : (b + 1) * VARS]


def make_rate(fields, geom, own, received, border, inner, weights):
    elems = geom.shape[1]
    faces = inner[0].shape[1]
    whole = pl.BlockSpec(memory_space=pltpu.VMEM)
    return pl.pallas_call(
        rate_kernel,
        grid=(faces // TILE // 2,),
        in_specs=[whole] * 22,
        out_specs=(whole, pl.BlockSpec(memory_space=pltpu.SMEM)),
        out_shape=(
            jax.ShapeDtypeStruct((BASIS, VARS, elems), F32),
            jax.ShapeDtypeStruct((1, 1), F32),
        ),
        scratch_shapes=[
            pltpu.VMEM((2 * ROWS, elems), BF16),
            pltpu.VMEM((2 * ROWS, elems), F32),
            pltpu.VMEM((elems, 2 * TILE), BF16),
            pltpu.VMEM((elems, 2 * TILE), BF16),
            pltpu.VMEM((2 * ROWS, 1024), F32),
            pltpu.VMEM((2 * ROWS, 2 * TILE), BF16),
        ],
        name="rate",
    )(*fields, geom, own, *received, *border, *inner, *weights)


def body(
    conserved,
    cell_size,
    sound_speed,
    jacobian,
    derivative,
    restriction,
    lifting,
    vertex_velocity,
    share_index,
    elem_vertex,
    inner_elem,
    inner_face,
    inner_normal,
    slab_elem,
    slab_face,
    slab_normal,
    peer_elem,
    peer_face,
    peer_normal,
    peer_count,
):
    elems = conserved.shape[2]
    slabs = lax.axis_size("shock")
    up = [(i, i + 1) for i in range(slabs - 1)]
    down = [(i + 1, i) for i in range(slabs - 1)]

    shared = jax.ShapeDtypeStruct((8, 128), F32)
    to_lower, to_upper = pl.pallas_call(
        share_kernel,
        out_shape=(shared, shared),
        scratch_shapes=[pltpu.VMEM((8, vertex_velocity.shape[1]), F32)],
        name="share",
    )(vertex_velocity, share_index)
    from_lower = lax.ppermute(to_upper, "shock", up)
    from_upper = lax.ppermute(to_lower, "shock", down)
    w_elem, w_trace, w_flux, w_lift = make_weights(jacobian, derivative, restriction, lifting)
    geom, least = pl.pallas_call(
        mesh_kernel,
        out_shape=(
            jax.ShapeDtypeStruct((8, elems), F32),
            jax.ShapeDtypeStruct((slabs, 1, 128), F32),
        ),
        scratch_shapes=[pltpu.VMEM((8, vertex_velocity.shape[1] + 256), F32)],
        name="mesh",
    )(
        vertex_velocity,
        from_lower,
        from_upper,
        elem_vertex,
        cell_size.reshape(1, elems),
        sound_speed.reshape(1, elems),
    )
    slab_least = lax.all_to_all(least, "shock", split_axis=0, concat_axis=0, tiled=True)

    state = jnp.transpose(conserved, (1, 0, 2))
    first, second, third, own, slab_down, slab_up, peer_send = make_front(
        state, geom, slab_least, (slab_elem, slab_face, peer_elem, peer_face), w_elem, w_trace
    )
    slab_lower = lax.ppermute(slab_up, "shock", up)
    slab_upper = lax.ppermute(slab_down, "shock", down)
    peer_recv = lax.all_to_all(peer_send, "trans", split_axis=0, concat_axis=0, tiled=True)
    fourth = make_third(third, geom, w_elem)
    rate, step_size = make_rate(
        (first, second, third, fourth),
        geom,
        own,
        (slab_lower, slab_upper, peer_recv),
        (slab_elem, slab_face, slab_normal, peer_elem, peer_face, peer_normal, peer_count),
        (inner_elem, inner_face, inner_normal),
        (w_trace, w_flux, w_lift),
    )
    return (jnp.transpose(rate, (1, 0, 2)), step_size.reshape(()))


def solution(mesh):
    return jax.shard_map(
        body,
        mesh=mesh,
        in_specs=(
            P(None, None, ("shock", "trans")),
            P(("shock", "trans")),
            P(("shock", "trans")),
            P(),
            P(),
            P(),
            P(),
            P(None, ("shock", "trans")),
            P(None, ("shock", "trans")),
            P(None, ("shock", "trans")),
            P(None, ("shock", "trans")),
            P(None, ("shock", "trans")),
            P(None, ("shock", "trans")),
            P(None, ("shock", "trans")),
            P(None, ("shock", "trans")),
            P(None, None, ("shock", "trans")),
            P(None, ("shock", "trans")),
            P(None, ("shock", "trans")),
            P(None, None, ("shock", "trans")),
            P(None, ("shock", "trans")),
        ),
        out_specs=(P(None, None, ("shock", "trans")), P()),
        check_vma=False,
    )
```

```python
import functools

import jax
import jax.numpy as jnp
import numpy as np
from jax import lax
from jax.experimental import pallas as pl
from jax.experimental.pallas import tpu as pltpu
from jax.sharding import PartitionSpec as P

HIGHEST_PREC = lax.Precision.HIGHEST
CFL_NUMBER = 0.3
BF16 = jnp.bfloat16
F32 = jnp.float32

VARS = 11
BASIS = 10
FACE = 6
ROWS = 112
TROWS = 72
ELEM_BLOCK = 256
TILE = 1024
CHUNK = 512


def expansion_tables():
    rows = np.arange(ROWS)
    outer = np.zeros((ROWS, 16), np.float32)
    inner = np.zeros((ROWS, 16), np.float32)
    live = rows < VARS * BASIS
    outer[rows[live], rows[live] // VARS] = 1.0
    inner[rows[live], rows[live] % VARS] = 1.0
    face_live = (np.arange(TROWS) < VARS * FACE).astype(np.float32)[:, None]
    outer_face = outer[:TROWS] * face_live
    inner_face = inner[:TROWS] * face_live
    thrice = lambda matrix: np.tile(matrix, (1, 3))
    bound = np.zeros((TROWS, ROWS), np.float32)
    bound[VARS * FACE, VARS * BASIS] = 1.0
    return (
        thrice(outer.T),
        thrice(inner.T),
        thrice(outer_face.T),
        thrice(inner_face.T),
        thrice(inner @ inner.T),
        thrice(inner_face @ inner.T),
        thrice(inner @ inner_face.T),
        thrice(outer_face @ outer_face.T),
        thrice(bound),
    )


def exact_dot(left, right, contract=((1,), (0,))):
    return lax.dot_general(
        left, right, (contract, ((), ())), precision=HIGHEST_PREC, preferred_element_type=F32
    )


def split3_cols(wide):
    third = wide.shape[1] // 3
    high = wide.astype(BF16).astype(F32)
    lane = lax.broadcasted_iota(jnp.int32, wide.shape, 1)
    return jnp.where(lane < 2 * third, high, wide - high).astype(BF16)


def weights_kernel(
    jac, der, res, lif, outer3, inner3, outer_face3, inner_face3, var_elem, var_trace, var_lift,
    basis_face, bound, w_elem, w_trace, w_flux, w_lift, small, wide_a, wide_b, face_a,
):
    small[...] = jnp.zeros_like(small)
    wide_a[...] = jnp.zeros_like(wide_a)
    wide_b[...] = jnp.zeros_like(wide_b)
    face_a[...] = jnp.zeros_like(face_a)
    for d in range(3):
        small[16 * d : 16 * d + VARS, 0:VARS] = jac[:, d, :]
        small[48 + 16 * d : 48 + 16 * d + BASIS, 0:BASIS] = der[:, d, :]
    for k in range(4):
        small[96 + 16 * k : 96 + 16 * k + FACE, 0:BASIS] = res[:, k, :]
        small[160 + 16 * k : 160 + 16 * k + FACE, 0:BASIS] = lif[:, k, :]
    jac_cols = exact_dot(small[0:48, :], inner3[...])
    jac_face_cols = exact_dot(small[0:48, :], inner_face3[...])
    other_cols = exact_dot(small[48:160, :], outer3[...])

    def repeat_rows(cols, first, target, count):
        for b in range(count):
            target[b * VARS : (b + 1) * VARS, :] = jnp.broadcast_to(
                cols[first + b : first + b + 1], (VARS, cols.shape[1])
            )

    def tile_rows(cols, first, target, count):
        for b in range(count):
            target[b * VARS : (b + 1) * VARS, :] = cols[first : first + VARS]

    total = None
    for d in range(3):
        repeat_rows(other_cols, 16 * d, wide_a, BASIS)
        tile_rows(jac_cols, 16 * d, wide_b, BASIS)
        term = wide_a[...] * wide_b[...]
        total = term if total is None else total + term
        w_elem[(d + 1) * ROWS : (d + 2) * ROWS, :] = split3_cols(wide_a[...] * var_elem[...])
        tile_rows(jac_face_cols, 16 * d, face_a, FACE)
        w_flux[d * TROWS : (d + 1) * TROWS, :] = split3_cols(face_a[0:TROWS] * basis_face[...])
    w_elem[0:ROWS, :] = split3_cols(total)
    for k in range(4):
        repeat_rows(other_cols, 48 + 16 * k, wide_a, FACE)
        w_trace[k * TROWS : (k + 1) * TROWS, :] = split3_cols(
            wide_a[0:TROWS] * var_trace[...] + bound[...]
        )
        lif_cols = exact_dot(
            small[160 + 16 * k : 176 + 16 * k, :], outer_face3[...], ((0,), (0,))
        )
        repeat_rows(lif_cols, 0, face_a, BASIS)
        w_lift[k * ROWS : (k + 1) * ROWS, :] = split3_cols(face_a[...] * var_lift[...])


def make_weights(jacobian, derivative, restriction, lifting):
    tables = [jnp.asarray(table) for table in expansion_tables()]
    return pl.pallas_call(
        weights_kernel,
        out_shape=(
            jax.ShapeDtypeStruct((4 * ROWS, 3 * ROWS), BF16),
            jax.ShapeDtypeStruct((4 * TROWS, 3 * ROWS), BF16),
            jax.ShapeDtypeStruct((3 * TROWS, 3 * TROWS), BF16),
            jax.ShapeDtypeStruct((4 * ROWS, 3 * TROWS), BF16),
        ),
        scratch_shapes=[
            pltpu.VMEM((224, 16), F32),
            pltpu.VMEM((ROWS, 3 * ROWS), F32),
            pltpu.VMEM((ROWS, 3 * ROWS), F32),
            pltpu.VMEM((ROWS, 3 * TROWS), F32),
        ],
        cost_estimate=pl.CostEstimate(flops=4_000_000, bytes_accessed=2_000_000, transcendentals=0),
        name="weights",
    )(
        jnp.transpose(jacobian, (1, 0, 2)),
        jnp.transpose(derivative, (1, 0, 2)),
        jnp.transpose(restriction, (1, 0, 2)),
        jnp.transpose(lifting, (2, 0, 1)),
        *tables,
    )


def lane_gather(table, tiles, index_row):
    wide = jnp.broadcast_to(index_row, (8, 128))
    low = wide & 127
    high = lax.shift_right_logical(wide, 7)
    picked = jnp.take_along_axis(table[:, 0:128], low, axis=1)
    for t in range(1, tiles):
        other = jnp.take_along_axis(table[:, t * 128 : (t + 1) * 128], low, axis=1)
        picked = jnp.where(high == t, other, picked)
    return picked


def share_kernel(velocity, share, to_lower, to_upper, table):
    table[...] = jnp.zeros_like(table)
    table[0:3, :] = velocity[...]
    tiles = velocity.shape[1] // 128
    to_lower[...] = lane_gather(table, tiles, share[0:1, :])
    to_upper[...] = lane_gather(table, tiles, share[1:2, :])


def mesh_kernel(
    velocity, from_lower, from_upper, corners, sizes, sounds, after, geom, least, table
):
    del after
    own = velocity.shape[1]
    table[...] = jnp.zeros_like(table)
    table[0:3, 0:own] = velocity[...]
    table[:, own : own + 128] = from_lower[...]
    table[:, own + 128 : own + 256] = from_upper[...]
    tiles = (own + 256) // 128
    elems = corners.shape[1]
    for j in range(elems // 128):
        cols = slice(j * 128, (j + 1) * 128)
        total = None
        for corner in range(4):
            value = lane_gather(table, tiles, corners[corner : corner + 1, cols])
            total = value if total is None else total + value
        geom[:, cols] = total * 0.25
    moves = jnp.abs(geom[0:3, :])
    bound = sounds[...] + moves[0:1] + moves[1:2] + moves[2:3]
    geom[3:4, :] = bound
    geom[4:5, :] = 1.0 / sizes[...]
    least[...] = jnp.broadcast_to(
        jnp.min(sizes[...] / bound, axis=1, keepdims=True)[None], least.shape
    )


def split3_rows(value):
    high = value.astype(BF16)
    low = (value - high.astype(F32)).astype(BF16)
    return jnp.concatenate([high, low, high], axis=0)


def split2_rows(value):
    high = value.astype(BF16)
    low = (value - high.astype(F32)).astype(BF16)
    return jnp.concatenate([high, low], axis=0)


def apply_operator(pieces, geom, w_elem, cols):
    parts = jnp.dot(w_elem[...], pieces, preferred_element_type=F32)
    return (
        parts[0:ROWS]
        - geom[0:1, cols] * parts[ROWS : 2 * ROWS]
        - geom[1:2, cols] * parts[2 * ROWS : 3 * ROWS]
        - geom[2:3, cols] * parts[3 * ROWS : 4 * ROWS]
    ) * geom[4:5, cols]


def third_kernel(l2_ref, geom, w_elem, l3_out):
    l3_out[...] = apply_operator(split3_rows(l2_ref[...]), geom, w_elem, slice(None))


def make_third(second, geom, w_elem):
    elems = geom.shape[1]
    return pl.pallas_call(
        third_kernel,
        grid=(elems // CHUNK,),
        in_specs=[
            pl.BlockSpec((ROWS, CHUNK), lambda i: (0, i)),
            pl.BlockSpec((8, CHUNK), lambda i: (0, i)),
            pl.BlockSpec((4 * ROWS, 3 * ROWS), lambda i: (0, 0)),
        ],
        out_specs=pl.BlockSpec((ROWS, CHUNK), lambda i: (0, i)),
        out_shape=jax.ShapeDtypeStruct((ROWS, elems), F32),
        cost_estimate=pl.CostEstimate(
            flops=2 * 448 * 336 * elems, bytes_accessed=2_000_000, transcendentals=0
        ),
        name="third",
    )(second, geom, w_elem)


def build_selection(index_row, select):
    count = index_row.shape[1]
    low = index_row & (ELEM_BLOCK - 1)
    high = lax.shift_right_logical(index_row, 8)
    place = lax.broadcasted_iota(jnp.int32, (ELEM_BLOCK, count), 0)
    match = jnp.where(place == low, 1.0, 0.0).astype(BF16)
    for t in range(select.shape[0] // ELEM_BLOCK):
        here = jnp.where(high == t, 1.0, 0.0).astype(BF16)
        select[t * ELEM_BLOCK : (t + 1) * ELEM_BLOCK, :] = match * here


def choose(stacked, which, rows):
    value = stacked[0:rows]
    for k in range(1, 4):
        value = jnp.where(which == k, stacked[k * rows : (k + 1) * rows], value)
    return value


def traces_of(picked, which, w_trace):
    pieces = jnp.concatenate([picked, picked[0:ROWS]], axis=0)
    stacked = jnp.dot(w_trace[...], pieces, preferred_element_type=F32)
    return choose(stacked, which, TROWS)


def join_slab(ref):
    return jnp.concatenate([ref[0:1, :], ref[1:2, :]], axis=1)


def join_peers(value):
    wide = jnp.concatenate([value, value], axis=1)
    left = lax.broadcasted_iota(jnp.int32, (1, 128), 1) < 64
    return jnp.concatenate(
        [
            jnp.where(left, wide[2 * m : 2 * m + 1], wide[2 * m + 1 : 2 * m + 2])
            for m in range(4)
        ],
        axis=1,
    )


def front_kernel(
    state, geom, s_elem, s_face, p_elem, p_face, w_elem, w_trace, c_out, l1_out, l2_out, own,
    to_lower, to_upper, to_peer, table, select,
):
    step = pl.program_id(0)
    chunks = table.shape[1] // CHUNK

    @pl.when(step < chunks)
    def _():
        cols = pl.ds(pl.multiple_of(step * CHUNK, CHUNK), CHUNK)
        for b in range(BASIS):
            c_out[b * VARS : (b + 1) * VARS, :] = state[b]
        c_out[BASIS * VARS : BASIS * VARS + 1, :] = geom[3:4, cols]
        c_out[BASIS * VARS + 1 : ROWS, :] = jnp.zeros((1, CHUNK), F32)
        pieces = split3_rows(c_out[...])
        table[0 : 2 * ROWS, cols] = pieces[0 : 2 * ROWS]
        l1_out[...] = apply_operator(pieces, geom, w_elem, cols)
        pieces = split3_rows(l1_out[...])
        table[2 * ROWS : 4 * ROWS, cols] = pieces[0 : 2 * ROWS]
        l2_out[...] = apply_operator(pieces, geom, w_elem, cols)
        table[4 * ROWS : 6 * ROWS, cols] = split2_rows(l2_out[...])
        index_row = jnp.where(step == 0, join_slab(s_elem), join_peers(p_elem[...]))
        half = select.at[:, pl.ds(pl.multiple_of(jnp.minimum(step, 1) * 512, 512), 512)]

        @pl.when(step < 2)
        def _():
            build_selection(index_row, half)

    def border(half, which):
        picked = jnp.dot(table[...], half[...], preferred_element_type=F32).astype(BF16)
        own[3 * TROWS :, :] = jnp.zeros((8, own.shape[1]), F32)
        for i in range(3):
            own[i * TROWS : (i + 1) * TROWS, :] = traces_of(
                picked[2 * ROWS * i : 2 * ROWS * (i + 1)], which, w_trace
            )

    @pl.when(step == chunks)
    def _():
        border(select.at[:, 0:512], join_slab(s_face))
        to_lower[...] = own[0 : 3 * TROWS, 0:256]
        to_upper[...] = own[0 : 3 * TROWS, 256:512]

    @pl.when(step == chunks + 1)
    def _():
        border(select.at[:, 512:1024], join_peers(p_face[...]))
        left = lax.broadcasted_iota(jnp.int32, (ROWS, 128), 1) < 64
        for m in range(4):
            top = own[0:ROWS, m * 128 : (m + 1) * 128]
            bottom = own[ROWS : 2 * ROWS, m * 128 : (m + 1) * 128]
            to_peer[2 * m] = jnp.where(left, top, pltpu.roll(bottom, 64, 1))
            to_peer[2 * m + 1] = jnp.where(left, pltpu.roll(top, 64, 1), bottom)


def make_front(state, geom, border_index, w_elem, w_trace):
    elems = geom.shape[1]
    chunks = elems // CHUNK
    full = jax.ShapeDtypeStruct((ROWS, elems), F32)
    block = pl.BlockSpec((ROWS, CHUNK), lambda i: (0, jnp.minimum(i, chunks - 1)))
    whole = pl.BlockSpec(memory_space=pltpu.VMEM)
    return pl.pallas_call(
        front_kernel,
        grid=(chunks + 2,),
        in_specs=[pl.BlockSpec((BASIS, VARS, CHUNK), lambda i: (0, 0, jnp.minimum(i, chunks - 1)))]
        + [whole] * 7,
        out_specs=[
            block,
            block,
            block,
            pl.BlockSpec((2 * ROWS, 512), lambda i: (0, jnp.maximum(i - chunks, 0))),
            whole,
            whole,
            whole,
        ],
        out_shape=[full] * 3
        + [
            jax.ShapeDtypeStruct((2 * ROWS, 1024), F32),
            jax.ShapeDtypeStruct((3 * TROWS, 256), F32),
            jax.ShapeDtypeStruct((3 * TROWS, 256), F32),
            jax.ShapeDtypeStruct((8, ROWS, 128), F32),
        ],
        scratch_shapes=[pltpu.VMEM((6 * ROWS, elems), BF16), pltpu.VMEM((elems, 1024), BF16)],
        name="front",
    )(state, geom, *border_index, w_elem, w_trace)


def stamp_kernel(least, value, out):
    row = lax.broadcasted_iota(jnp.int32, value.shape, 1)
    lane = lax.broadcasted_iota(jnp.int32, value.shape, 2)
    out[...] = jnp.where((row == 7) & (lane >= 64), jnp.min(least[...]), value[...])


def make_stamp(least, to_peer):
    block = pl.BlockSpec((8, 8, 128), lambda i: (0, ROWS // 8 - 1, 0))
    return pl.pallas_call(
        stamp_kernel,
        grid=(1,),
        in_specs=[pl.BlockSpec(memory_space=pltpu.VMEM), block],
        out_specs=block,
        out_shape=jax.ShapeDtypeStruct(to_peer.shape, F32),
        input_output_aliases={1: 0},
        name="stamp",
    )(least, to_peer)


def flux_parts(own, theirs, normal, w_flux):
    jump = theirs - own
    bound = jnp.maximum(own[66:67], theirs[66:67])
    parts = jnp.dot(w_flux[...], split3_rows(jump), preferred_element_type=F32)
    central = (
        normal[0:1] * parts[0:TROWS]
        + normal[1:2] * parts[TROWS : 2 * TROWS]
        + normal[2:3] * parts[2 * TROWS : 3 * TROWS]
    )
    return central, bound * jump


def lift_values(values, which, w_lift):
    stacked = jnp.dot(w_lift[...], split3_rows(values), preferred_element_type=F32)
    return split2_rows(choose(stacked, which, ROWS))


def add_selected(pieces, select, total):
    total[...] += lax.dot_general(
        pieces, select[...], (((1,), (1,)), ((), ())), preferred_element_type=F32
    )


def combine(first, second, third, half, sixth):
    return first + half * second + sixth * third


def rate_kernel(
    c_any, l1_any, l2_any, l3_any, geom, own, from_lower, from_upper, from_peer, s_elem, s_face,
    s_normal, p_elem, p_face, p_normal, p_count, elem, face, normal, w_trace, w_flux, w_lift, out,
    step_out, table, total, even, odd, theirs, c_ref, l1_ref, l2_ref, l3_ref, arrived,
):
    step = pl.program_id(0)
    last_tile = elem.shape[1] // TILE - 1
    tau = CFL_NUMBER * jnp.min(from_peer[:, ROWS - 1 : ROWS, 64:128])
    half = -0.5 * tau
    sixth = tau * tau / 6.0

    def sides(tile):
        cols = pl.ds(pl.multiple_of(tile * TILE, TILE), TILE)
        index_row = jnp.concatenate([elem[0:1, cols], elem[1:2, cols]], axis=1)
        which = jnp.concatenate([face[0:1, cols], face[1:2, cols]], axis=1)
        return index_row, which

    def inner_values(tile, traces):
        cols = pl.ds(pl.multiple_of(tile * TILE, TILE), TILE)
        central, upwind = flux_parts(traces[:, 0:TILE], traces[:, TILE:], normal[:, cols], w_flux)
        return jnp.concatenate([0.5 * (central - upwind), 0.5 * (central + upwind)], axis=1)

    @pl.when(step == 0)
    def _():
        step_out[0, 0] = tau
        loads = [
            pltpu.make_async_copy(source, target, arrived.at[i])
            for i, (source, target) in enumerate(
                ((c_any, c_ref), (l1_any, l1_ref), (l2_any, l2_ref), (l3_any, l3_ref))
            )
        ]
        for load in loads:
            load.start()
        left = lax.broadcasted_iota(jnp.int32, (ROWS, 128), 1) < 64
        theirs[0 : 3 * TROWS, 0:256] = from_lower[...]
        theirs[0 : 3 * TROWS, 256:512] = from_upper[...]
        for m in range(4):
            cols = slice(512 + m * 128, 512 + (m + 1) * 128)
            one, two = from_peer[2 * m], from_peer[2 * m + 1]
            theirs[0:ROWS, cols] = jnp.where(left, one, pltpu.roll(two, 64, 1))
            theirs[ROWS : 2 * ROWS, cols] = jnp.where(left, pltpu.roll(one, 64, 1), two)
        slot = lax.broadcasted_iota(jnp.int32, (1, 128), 1)
        alive = jnp.concatenate(
            [
                jnp.where(
                    slot < 64,
                    jnp.where(slot < p_count[0:1, 2 * m : 2 * m + 1], 1.0, 0.0),
                    jnp.where(slot - 64 < p_count[0:1, 2 * m + 1 : 2 * m + 2], 1.0, 0.0),
                )
                for m in range(4)
            ],
            axis=1,
        )
        b_elem = jnp.concatenate([join_slab(s_elem), join_peers(p_elem[...])], axis=1)
        b_face = jnp.concatenate([join_slab(s_face), join_peers(p_face[...])], axis=1)
        b_live = jnp.concatenate([jnp.ones((1, 512), F32), alive], axis=1)
        b_normal = jnp.concatenate(
            [
                jnp.concatenate([join_slab(s_normal.at[d]), join_peers(p_normal[d])], axis=1)
                for d in range(3)
            ],
            axis=0,
        )
        build_selection(b_elem, odd.at[:, 0:1024])
        index_row, _ = sides(0)
        build_selection(index_row, even)

        def merged(ref):
            return combine(
                ref[0:TROWS], ref[TROWS : 2 * TROWS], ref[2 * TROWS : 3 * TROWS], half, sixth
            )

        central, upwind = flux_parts(merged(own), merged(theirs), b_normal, w_flux)
        values = (0.5 * (central - upwind)) * b_live
        total[...] = lax.dot_general(
            lift_values(values, b_face, w_lift),
            odd[:, 0:1024],
            (((1,), (1,)), ((), ())),
            preferred_element_type=F32,
        )
        for load in loads:
            load.wait()
        for j in range(c_ref.shape[1] // CHUNK):
            cols = slice(j * CHUNK, (j + 1) * CHUNK)
            table[:, cols] = split2_rows(
                combine(c_ref[:, cols], l1_ref[:, cols], l2_ref[:, cols], half, sixth)
            )
    for parity in range(2):
        tile = 2 * step + parity
        cur, nxt = (even, odd) if parity == 0 else (odd, even)
        picked = jnp.dot(table[...], cur[...], preferred_element_type=F32).astype(BF16)
        index_next, _ = sides(jnp.minimum(tile + 1, last_tile))
        build_selection(index_next, nxt)
        _, which = sides(tile)
        values = inner_values(tile, traces_of(picked, which, w_trace))
        add_selected(lift_values(values, which, w_lift), cur, total)
    @pl.when(step == pl.num_programs(0) - 1)
    def _():
        for j in range(c_ref.shape[1] // CHUNK):
            cols = slice(j * CHUNK, (j + 1) * CHUNK)
            summed = total[0:ROWS, cols] + total[ROWS : 2 * ROWS, cols]
            volume = combine(l1_ref[:, cols], l2_ref[:, cols], l3_ref[:, cols], half, sixth)
            rate = -(volume + summed * geom[4:5, cols])
            for b in range(BASIS):
                out[b, :, cols] = rate[b * VARS : (b + 1) * VARS]


def make_rate(fields, geom, own, received, border, inner, weights):
    elems = geom.shape[1]
    faces = inner[0].shape[1]
    whole = pl.BlockSpec(memory_space=pltpu.VMEM)
    return pl.pallas_call(
        rate_kernel,
        grid=(faces // TILE // 2,),
        in_specs=[pl.BlockSpec(memory_space=pl.ANY)] * 4 + [whole] * 18,
        out_specs=(whole, pl.BlockSpec(memory_space=pltpu.SMEM)),
        out_shape=(
            jax.ShapeDtypeStruct((BASIS, VARS, elems), F32),
            jax.ShapeDtypeStruct((1, 1), F32),
        ),
        scratch_shapes=[
            pltpu.VMEM((2 * ROWS, elems), BF16),
            pltpu.VMEM((2 * ROWS, elems), F32),
            pltpu.VMEM((elems, 2 * TILE), BF16),
            pltpu.VMEM((elems, 2 * TILE), BF16),
            pltpu.VMEM((2 * ROWS, 1024), F32),
            pltpu.VMEM((ROWS, elems), F32),
            pltpu.VMEM((ROWS, elems), F32),
            pltpu.VMEM((ROWS, elems), F32),
            pltpu.VMEM((ROWS, elems), F32),
            pltpu.SemaphoreType.DMA((4,)),
        ],
        name="rate",
    )(*fields, geom, own, *received, *border, *inner, *weights)


def body(
    conserved,
    cell_size,
    sound_speed,
    jacobian,
    derivative,
    restriction,
    lifting,
    vertex_velocity,
    share_index,
    elem_vertex,
    inner_elem,
    inner_face,
    inner_normal,
    slab_elem,
    slab_face,
    slab_normal,
    peer_elem,
    peer_face,
    peer_normal,
    peer_count,
):
    elems = conserved.shape[2]
    slabs = lax.axis_size("shock")
    up = [(i, i + 1) for i in range(slabs - 1)]
    down = [(i + 1, i) for i in range(slabs - 1)]

    shared = jax.ShapeDtypeStruct((8, 128), F32)
    to_lower, to_upper = pl.pallas_call(
        share_kernel,
        out_shape=(shared, shared),
        scratch_shapes=[pltpu.VMEM((8, vertex_velocity.shape[1]), F32)],
        name="share",
    )(vertex_velocity, share_index)
    from_lower = lax.ppermute(to_upper, "shock", up)
    from_upper = lax.ppermute(to_lower, "shock", down)
    w_elem, w_trace, w_flux, w_lift = make_weights(jacobian, derivative, restriction, lifting)
    geom, least = pl.pallas_call(
        mesh_kernel,
        out_shape=(
            jax.ShapeDtypeStruct((8, elems), F32),
            jax.ShapeDtypeStruct((slabs, 1, 128), F32),
        ),
        in_specs=[pl.BlockSpec(memory_space=pltpu.VMEM)] * 6 + [pl.BlockSpec(memory_space=pl.ANY)],
        scratch_shapes=[pltpu.VMEM((8, vertex_velocity.shape[1] + 256), F32)],
        name="mesh",
    )(
        vertex_velocity,
        from_lower,
        from_upper,
        elem_vertex,
        cell_size.reshape(1, elems),
        sound_speed.reshape(1, elems),
        w_flux,
    )
    slab_least = lax.all_to_all(least, "shock", split_axis=0, concat_axis=0, tiled=True)

    state = jnp.transpose(conserved, (1, 0, 2))
    first, second, third, own, slab_down, slab_up, peer_send = make_front(
        state, geom, (slab_elem, slab_face, peer_elem, peer_face), w_elem, w_trace
    )
    slab_lower = lax.ppermute(slab_up, "shock", up)
    slab_upper = lax.ppermute(slab_down, "shock", down)
    peer_send = make_stamp(slab_least, peer_send)
    peer_recv = lax.all_to_all(peer_send, "trans", split_axis=0, concat_axis=0, tiled=True)
    fourth = make_third(third, geom, w_elem)
    in_vmem = lambda value: pltpu.with_memory_space_constraint(value, pltpu.VMEM)
    slab_lower, slab_upper, peer_recv = in_vmem(slab_lower), in_vmem(slab_upper), in_vmem(peer_recv)
    rate, step_size = make_rate(
        (first, second, third, fourth),
        geom,
        own,
        (slab_lower, slab_upper, peer_recv),
        (slab_elem, slab_face, slab_normal, peer_elem, peer_face, peer_normal, peer_count.reshape(1, -1)),
        (inner_elem, inner_face, inner_normal),
        (w_trace, w_flux, w_lift),
    )
    return (jnp.transpose(rate, (1, 0, 2)), step_size.reshape(()))


def solution(mesh):
    return jax.shard_map(
        body,
        mesh=mesh,
        in_specs=(
            P(None, None, ("shock", "trans")),
            P(("shock", "trans")),
            P(("shock", "trans")),
            P(),
            P(),
            P(),
            P(),
            P(None, ("shock", "trans")),
            P(None, ("shock", "trans")),
            P(None, ("shock", "trans")),
            P(None, ("shock", "trans")),
            P(None, ("shock", "trans")),
            P(None, ("shock", "trans")),
            P(None, ("shock", "trans")),
            P(None, ("shock", "trans")),
            P(None, None, ("shock", "trans")),
            P(None, ("shock", "trans")),
            P(None, ("shock", "trans")),
            P(None, None, ("shock", "trans")),
            P(None, ("shock", "trans")),
        ),
        out_specs=(P(None, None, ("shock", "trans")), P()),
        check_vma=False,
    )
```
